32 devices in a mesh: pix: 16 (over z, y, core), frm: 2 (over x).
Axes of the slice: x: 2, y: 2, z: 4, core: 2. Of those that a mesh axis runs over, the one named last changes fastest.
Arguments:
- frames: bfloat16 [65536, 768], P('pix', 'frm'), may hold values from 0 to 6
- footprints: bfloat16 [65536, 192], P('pix'), may hold values from 0 to 0.024414062
- support: int32 [4096, 192], P('pix'), may hold values 0 or 1
- traces: float32 [1024, 768], P('pix', 'frm'), may hold values from 0 to 2
- block_order: int32 [16, 2], replicated, may hold values from 0 to 1, each once within a row
Outputs:
- refined: bfloat16 [65536, 192], P(('pix', 'frm'))
- updated: float32 [1024, 768], P('pix', 'frm')
The draws below stay inside these ranges and needn't reach their ends.
Inputs may be any that keep to these rules, and one draw needn't show every extreme that they name: `block_order`: each row lists every block index of a slab once.
All inputs are finite; a program needn't handle non-finite values. No bound on the sum of `support` on one device may be relied on, other than what follows from the above.
Results may differ from the reference program's by a relative error of at most 0.0036.
Values may be sent and summed in bfloat16 or wider, within the bound.
A program may use at most 64 MiB of HBM per device.

```python
import math
import jax
import jax.numpy as jnp
from jax import lax

KO = 64
BLOCK = 32
TILE = 16
PD = 4096
OWNERS = 16
PIXELS = 65536
TOTAL_FRAMES = 768
K = 1024
B_OWN = 2


def draw_frames(key, part):
    row_key, noise_key = jax.random.split(jax.random.fold_in(key, 7))
    level = jax.random.uniform(row_key, (PIXELS, 1), jnp.float32)
    scale = 0.35 * jnp.exp(level * math.log(8.0))
    noise = jax.random.uniform(noise_key, (PIXELS, TOTAL_FRAMES), jnp.float32, 0.0, 2.0)
    return (scale * noise).astype(jnp.bfloat16)


def with_ends(entries, rng, low, largest):
    index_at = [jax.random.randint(jax.random.fold_in(rng, axis), (), 0, length) for axis, length in enumerate(entries.shape)]
    main_axis = entries.shape.index(max(entries.shape))
    beside = index_at[:main_axis] + [(index_at[main_axis] + 1) % entries.shape[main_axis]] + index_at[main_axis + 1:]
    return entries.at[tuple(index_at)].set(low).at[tuple(beside)].set(largest)


def shard_levels(stream_key, dims, pieces, least, top_value):
    loudness, own = 1.0, jax.random.fold_in(stream_key, 6)
    for position, shards_of in pieces:
        heights = jnp.exp(jax.random.uniform(jax.random.fold_in(own, position), (shards_of,), jnp.float32, least / len(pieces), top_value / len(pieces)))
        loudness = loudness * jnp.repeat(heights, dims[position] // shards_of).reshape([-1 if axis == position else 1 for axis in range(len(dims))])
    return loudness


def setup_inputs(seed: int = 0) -> dict:
    splits = jax.random.split(jax.random.key(seed), 6)
    frames = draw_frames(jax.random.fold_in(splits[5], 71), 0)
    footprints = jnp.clip(0.024414062 * jax.random.uniform(splits[1], (PIXELS, 3 * KO), jnp.float32) ** shard_levels(splits[1], (PIXELS, 3 * KO), ((0, 16),), -0.2, 0.2), 0.0, 0.024414062).astype(jnp.bfloat16)
    support = with_ends((jax.random.randint(splits[2], (PIXELS // TILE, 3 * KO), 0, 2) < 1).astype(jnp.int32), jax.random.fold_in(splits[2], 1), 0, 1)
    traces = jnp.clip(2.0 * jax.random.uniform(splits[3], (K, TOTAL_FRAMES), jnp.float32) ** shard_levels(splits[3], (K, TOTAL_FRAMES), ((0, 16), (1, 2)), -0.2, 0.2), 0.0, 2.0)
    block_order = jax.vmap(lambda own: jax.random.permutation(own, B_OWN))(jax.random.split(splits[4], OWNERS)).reshape((OWNERS, B_OWN)).astype(jnp.int32)
    return {"frames": frames, "footprints": footprints, "support": support, "traces": traces, "block_order": block_order}


highest = lax.Precision.HIGHEST


def slab_masks(support_slab, slab_id):
    expanded = jnp.repeat(support_slab, TILE, axis=0).astype(jnp.float32)
    window_of = jnp.arange(3 * KO, dtype=jnp.int32) // KO
    usable = jnp.where(window_of == 0, slab_id > 0, jnp.where(window_of == 2, slab_id < OWNERS - 1, True))
    return expanded * usable.astype(jnp.float32)[None, :]


def trace_block(current, window, drive_rows, coupling, block_id):
    row_start = (block_id * BLOCK).astype(jnp.int32)
    band_rows = lax.dynamic_slice_in_dim(coupling, row_start, BLOCK, 0)
    diagonal = jnp.diagonal(lax.dynamic_slice_in_dim(band_rows, 2 * KO + row_start, BLOCK, 1))
    product = jnp.dot(band_rows, window, precision=highest)
    target = lax.dynamic_slice_in_dim(drive_rows, row_start, BLOCK, 0)
    before = lax.dynamic_slice_in_dim(current, row_start, BLOCK, 0)
    after = jnp.maximum(before + (target - product) / (diagonal[:, None] + 1.0), 0.0)
    return lax.dynamic_update_slice_in_dim(current, after, row_start, 0)


def reference(frames, footprints, support, traces, block_order):
    frame_slabs = frames.reshape(OWNERS, PD, TOTAL_FRAMES)
    foot_slabs = footprints.reshape(OWNERS, PD, 3 * KO)
    support_slabs = support.reshape(OWNERS, PD // TILE, 3 * KO)
    slab_ids = jnp.arange(OWNERS, dtype=jnp.int32)

    def project(inputs):
        frame_slab, foot_slab, support_slab, slab_id = inputs
        active = (foot_slab.astype(jnp.float32) * slab_masks(support_slab, slab_id)).astype(jnp.bfloat16)
        active_f = active.astype(jnp.float32)
        loads = jnp.einsum("pk,pt->kt", active_f, frame_slab.astype(jnp.float32), precision=highest)
        correlations = jnp.einsum("pk,pj->kj", active_f, active_f, precision=highest)
        return loads, correlations

    loads, correlations = lax.map(project, (frame_slabs, foot_slabs, support_slabs, slab_ids))
    zero_load = jnp.zeros((1, KO, TOTAL_FRAMES), jnp.float32)
    from_right = jnp.concatenate([loads[1:, :KO], zero_load], axis=0)
    from_left = jnp.concatenate([zero_load, loads[:-1, 2 * KO:]], axis=0)
    drive = loads[:, KO:2 * KO] + from_right + from_left
    zero_gram = jnp.zeros((1, KO, 3 * KO), jnp.float32)
    right_rows = jnp.concatenate([correlations[1:, :KO], zero_gram], axis=0)
    left_rows = jnp.concatenate([zero_gram, correlations[:-1, 2 * KO:]], axis=0)
    coupling = jnp.pad(correlations[:, KO:2 * KO], ((0, 0), (0, 0), (KO, KO)))
    coupling = coupling + jnp.pad(right_rows, ((0, 0), (0, 0), (2 * KO, 0)))
    coupling = coupling + jnp.pad(left_rows, ((0, 0), (0, 0), (0, 2 * KO)))

    current = traces.reshape(OWNERS, KO, TOTAL_FRAMES)
    for step in range(B_OWN):
        padded = jnp.pad(current, ((2, 2), (0, 0), (0, 0)))
        windows = jnp.stack([padded[i:i + OWNERS] for i in range(5)], axis=1).reshape(OWNERS, 5 * KO, TOTAL_FRAMES)
        current = jax.vmap(trace_block)(current, windows, drive, coupling, block_order[:, step])

    near_all = jnp.pad(current.astype(jnp.bfloat16), ((1, 1), (0, 0), (0, 0)))

    def refine(inputs):
        frame_slab, foot_slab, support_slab, slab_id = inputs
        near = lax.dynamic_slice_in_dim(near_all, slab_id, 3, 0).reshape(3 * KO, TOTAL_FRAMES).astype(jnp.float32)
        mixing = jnp.einsum("pt,kt->pk", frame_slab.astype(jnp.float32), near, precision=highest)
        gram = jnp.einsum("kt,jt->kj", near, near, precision=highest)
        keep = slab_masks(support_slab, slab_id)
        shaped = foot_slab.astype(jnp.float32) * keep
        for step in range(B_OWN):
            slab_near = jnp.clip(slab_id - 1 + jnp.arange(3, dtype=jnp.int32), 0, OWNERS - 1)
            picked = block_order[slab_near, step]
            columns = (jnp.arange(3, dtype=jnp.int32)[:, None] * KO + picked[:, None] * BLOCK
                       + jnp.arange(BLOCK, dtype=jnp.int32)[None, :]).reshape(-1)
            gram_cols = jnp.take(gram, columns, axis=1)
            diagonal = jnp.diagonal(jnp.take(gram_cols, columns, axis=0))
            before = jnp.take(shaped, columns, axis=1)
            target = jnp.take(mixing, columns, axis=1)
            keep_cols = jnp.take(keep, columns, axis=1)
            product = jnp.dot(shaped, gram_cols, precision=highest)
            after = jnp.maximum(before + (target - product) / (diagonal[None, :] + 1.0), 0.0) * keep_cols
            shaped = shaped.at[:, columns].set(after)
        return shaped.astype(jnp.bfloat16)

    refined = lax.map(refine, (frame_slabs, foot_slabs, support_slabs, slab_ids))
    return refined.reshape(PIXELS, 3 * KO), current.reshape(K, TOTAL_FRAMES)
```

```python
import functools

import jax
import jax.numpy as jnp
from jax import lax
from jax.experimental import pallas as pl
from jax.experimental.pallas import tpu as pltpu
from jax.sharding import PartitionSpec as P

BLOCK = 32
TILE = 16
MESH = pl.DeviceIdType.MESH
OFFSETS = (-2, -1, 1, 2)
f32, bf16 = jnp.float32, jnp.bfloat16


def dot(a, b, dims=((1,), (0,))):
    return lax.dot_general(a, b, (dims, ((), ())), preferred_element_type=f32)


def halves(x):
    high = x.astype(bf16)
    return high, (x - high.astype(f32)).astype(bf16)


def kernel(
    owners, shares, order_ref, frames_ref, foot_ref, support_ref, traces_ref, refined_ref, updated_ref,
    act, keep, pc, side, win, blk_out, blk_in, near, gram_own, gram_in, part_own, part_out, part_in,
    a_send, a_recv, b_send, b_recv, c_send, c_recv, d_send, d_recv, g_send, g_recv, f_send, f_recv,
):
    slab, mine = lax.axis_index("pix"), lax.axis_index("frm")
    pixels, frames_here = frames_ref.shape
    width = traces_ref.shape[0]
    three = 3 * width
    sweeps = width // BLOCK
    share_rows = pixels // shares
    barrier = pltpu.get_barrier_semaphore()

    def present(offset):
        return slab + offset >= 0 if offset < 0 else slab + offset < owners

    def slot(offset):
        return OFFSETS.index(offset)

    def partner(d):
        return lax.rem(mine + d, shares)

    for offset in OFFSETS:
        @pl.when(present(offset))
        def _():
            pl.semaphore_signal(barrier, inc=1, device_id=(slab + offset, mine), device_id_type=MESH)

        @pl.when(jnp.logical_not(present(offset)))
        def _():
            row = (2 + offset) * width
            win[row : row + width, :] = jnp.zeros((width, frames_here), f32)
            for step in range(sweeps - 1):
                blk_in[step, slot(offset)] = jnp.zeros((BLOCK, frames_here), f32)
            if abs(offset) == 1:
                at = 0 if offset < 0 else 1
                side[at] = jnp.zeros(side.shape[1:], f32)
                row = (1 + offset) * width
                near[row : row + width, :] = jnp.zeros((width, frames_here), bf16)
    for d in range(1, shares):
        pl.semaphore_signal(barrier, inc=1, device_id=(slab, partner(d)), device_id_type=MESH)

    win[2 * width : 3 * width, :] = traces_ref[...]

    peers = jnp.minimum(slab, 2) + jnp.minimum(owners - 1 - slab, 2) + shares - 1
    pl.semaphore_wait(barrier, peers)

    def send_traces(offset):
        row = (2 - offset) * width
        k = slot(-offset)
        return pltpu.make_async_remote_copy(
            src_ref=traces_ref, dst_ref=win.at[pl.ds(row, width)], send_sem=a_send.at[k],
            recv_sem=a_recv.at[k], device_id=(slab + offset, mine), device_id_type=MESH)

    def send_side(offset):
        at = 1 if offset < 0 else 0
        row = 0 if offset < 0 else 2 * width
        return pltpu.make_async_remote_copy(
            src_ref=pc.at[pl.ds(row, width)], dst_ref=side.at[at], send_sem=b_send.at[at],
            recv_sem=b_recv.at[at], device_id=(slab + offset, mine), device_id_type=MESH)

    def send_block(step, offset):
        k = slot(-offset)
        return pltpu.make_async_remote_copy(
            src_ref=blk_out.at[step], dst_ref=blk_in.at[step, k], send_sem=c_send.at[step, k],
            recv_sem=c_recv.at[step, k], device_id=(slab + offset, mine), device_id_type=MESH)

    def send_near(offset):
        at = 1 if offset < 0 else 0
        row = (1 - offset) * width
        return pltpu.make_async_remote_copy(
            src_ref=near.at[pl.ds(width, width)], dst_ref=near.at[pl.ds(row, width)], send_sem=d_send.at[at],
            recv_sem=d_recv.at[at], device_id=(slab + offset, mine), device_id_type=MESH)

    def send_gram(d):
        return pltpu.make_async_remote_copy(
            src_ref=gram_own, dst_ref=gram_in.at[d - 1], send_sem=g_send.at[d - 1],
            recv_sem=g_recv.at[d - 1], device_id=(slab, partner(d)), device_id_type=MESH)

    pieces, rows_each = part_out.shape[1], part_out.shape[3]

    def send_part(d, piece):
        return pltpu.make_async_remote_copy(
            src_ref=part_out.at[d - 1, piece], dst_ref=part_in.at[d - 1, piece], send_sem=f_send.at[d - 1, piece],
            recv_sem=f_recv.at[d - 1, piece], device_id=(slab, partner(d)), device_id_type=MESH)

    def start(copy, offset):
        @pl.when(present(offset))
        def _():
            copy(offset).start()

    def arrive(copy, offset):
        @pl.when(present(-offset))
        def _():
            copy(offset).wait_recv()

    def left(copy, offset):
        @pl.when(present(offset))
        def _():
            copy(offset).wait_send()

    for offset in OFFSETS:
        start(send_traces, offset)

    line = lax.broadcasted_iota(jnp.int32, (three, 1), 0)
    window_of = line // width
    usable = jnp.where(
        window_of == 0, (slab > 0).astype(f32), jnp.where(window_of == 2, (slab < owners - 1).astype(f32), 1.0))
    supported = (support_ref[...].astype(f32) * usable).astype(bf16)

    chunk = min(pixels, 512)
    tiles = support_ref.shape[1]
    pc[...] = jnp.zeros(pc.shape, f32)
    tile_of = lax.broadcasted_iota(jnp.int32, (tiles, chunk), 1) // TILE
    tile_is = lax.broadcasted_iota(jnp.int32, (tiles, chunk), 0)

    def project(c, carry):
        rows = pl.ds(pl.multiple_of(c * chunk, chunk), chunk)
        spread = (tile_is == tile_of + c * (chunk // TILE)).astype(f32).astype(bf16)
        mask = dot(supported, spread).astype(bf16)
        active = foot_ref[:, rows] * mask
        keep[:, rows] = mask
        act[:, rows] = active
        pc[:, :frames_here] += dot(active, frames_ref[rows, :])
        pc[:, frames_here : frames_here + three] += dot(active, active, ((1,), (1,)))
        return carry

    lax.fori_loop(0, pixels // chunk, project, 0)
    for offset in (-1, 1):
        start(send_side, offset)
    for offset in OFFSETS:
        arrive(send_traces, offset)
    for offset in (-1, 1):
        arrive(send_side, offset)

    own = pc[width : 2 * width, :]
    loads = own[:, :frames_here] + side[0][:, :frames_here] + side[1][:, :frames_here]
    parts = [side[0][:, frames_here : frames_here + three], own[:, frames_here : frames_here + three],
             side[1][:, frames_here : frames_here + three]]
    row = lax.broadcasted_iota(jnp.int32, (width, three), 0)
    column = lax.broadcasted_iota(jnp.int32, (width, three), 1)
    diagonal = jnp.zeros((width, 1), f32)
    stacked, tops = [], []
    for i, part in enumerate(parts):
        diagonal += jnp.sum(jnp.where(column == row + (2 - i) * width, part, 0.0), axis=1, keepdims=True)
        high, low = halves(part)
        tops.append(high)
        stacked.append(jnp.concatenate([high, low], axis=0))
    block_of = lax.broadcasted_iota(jnp.int32, (width, 1), 0) // BLOCK

    for step in range(sweeps):
        if step > 0:
            for offset in OFFSETS:
                arrive(functools.partial(send_block, step - 1), offset)
            for offset in OFFSETS:
                there = jnp.clip(slab + offset, 0, owners - 1)
                first = (2 + offset) * width
                news = jnp.concatenate([blk_in[step - 1, slot(offset)]] * sweeps, axis=0)
                win[first : first + width, :] = jnp.where(
                    block_of == order_ref[step - 1, there], news, win[first : first + width, :])
        high, low = halves(win[...])
        product = jnp.zeros((width, frames_here), f32)
        for i in range(3):
            span = slice(i * width, i * width + three)
            both = dot(stacked[i], high[span])
            product += both[:width] + both[width:] + dot(tops[i], low[span])
        before = win[2 * width : 3 * width, :]
        after = jnp.maximum(before + (loads - product) / (diagonal + 1.0), 0.0)
        picked = order_ref[step, slab]
        if step < sweeps - 1:
            block = jnp.zeros((BLOCK, frames_here), f32)
            for k in range(sweeps):
                block = jnp.where(picked == k, after[k * BLOCK : (k + 1) * BLOCK], block)
            blk_out[step] = block
            for offset in OFFSETS:
                start(functools.partial(send_block, step), offset)
        current = jnp.where(block_of == picked, after, before)
        if step < sweeps - 1:
            win[2 * width : 3 * width, :] = current
        else:
            near[width : 2 * width, :] = current.astype(bf16)
            for offset in (-1, 1):
                start(send_near, offset)
            updated_ref[...] = current

    for offset in (-1, 1):
        arrive(send_near, offset)
    traces_near = near[...]
    gram_here = dot(traces_near, traces_near, ((1,), (1,)))
    gram_own[...] = gram_here
    for d in range(1, shares):
        send_gram(d).start()
    both = jnp.concatenate(halves(gram_here), axis=0)

    def residual(first):
        rows = pl.ds(pl.multiple_of(first, rows_each), rows_each)
        fitted = dot(both, act[:, rows])
        return dot(traces_near, frames_ref[rows, :], ((1,), (1,))) - fitted[:three] - fitted[three:]

    for piece in range(pieces):
        for d in range(1, shares):
            part_out[d - 1, piece] = residual(partner(d) * share_rows + piece * rows_each).astype(bf16)
            send_part(d, piece).start()
    for piece in range(pieces):
        part_own[piece] = residual(mine * share_rows + piece * rows_each)

    gram = gram_here
    for d in range(1, shares):
        send_gram(d).wait_recv()
        gram += gram_in[d - 1]
    grow = lax.broadcasted_iota(jnp.int32, (three, three), 0)
    gcol = lax.broadcasted_iota(jnp.int32, (three, three), 1)
    rate = 1.0 / (jnp.sum(jnp.where(grow == gcol, gram, 0.0), axis=1, keepdims=True) + 1.0)
    gram_high, gram_low = halves(gram)
    gram_both = jnp.concatenate([gram_high, gram_low], axis=0)
    line_block = lax.rem(line, width) // BLOCK
    picks = []
    for step in range(sweeps):
        chosen = [order_ref[step, jnp.clip(slab - 1 + w, 0, owners - 1)] for w in range(3)]
        chosen = jnp.where(window_of == 0, chosen[0], jnp.where(window_of == 1, chosen[1], chosen[2]))
        picks.append(line_block == chosen)

    for piece in range(pieces):
        left_over = part_own[piece]
        for d in range(1, shares):
            send_part(d, piece).wait_recv()
            left_over += part_in[d - 1, piece].astype(f32)
        here = pl.ds(pl.multiple_of(mine * share_rows + piece * rows_each, rows_each), rows_each)
        shaped = act[:, here].astype(f32)
        mask = keep[:, here].astype(f32)
        for step in range(sweeps):
            after = jnp.where(picks[step], jnp.maximum(shaped + left_over * rate, 0.0) * mask, shaped)
            if step < sweeps - 1:
                moved, rest = halves(after - shaped)
                change = dot(gram_both, moved)
                left_over -= change[:three] + change[three:] + dot(gram_high, rest)
            shaped = after
        refined_ref[:, piece * rows_each : (piece + 1) * rows_each] = shaped.astype(bf16)

    for offset in OFFSETS:
        left(send_traces, offset)
        for step in range(sweeps - 1):
            left(functools.partial(send_block, step), offset)
    for offset in (-1, 1):
        left(send_side, offset)
        left(send_near, offset)
    for d in range(1, shares):
        send_gram(d).wait_send()
        for piece in range(pieces):
            send_part(d, piece).wait_send()


def shards(owners, shares, frames, footprints, support, traces, block_order):
    pixels, frames_here = frames.shape
    width = traces.shape[0]
    three = 3 * width
    rounds = max(width // BLOCK - 1, 1)
    share_rows = pixels // shares
    rows_each = min(share_rows, 512)
    pieces = share_rows // rows_each
    others = max(shares - 1, 1)
    side_width = -(-(frames_here + three) // 128) * 128
    vmem, dma = pltpu.VMEM, pltpu.SemaphoreType.DMA
    refined, updated = pl.pallas_call(
        functools.partial(kernel, owners, shares),
        out_shape=(
            jax.ShapeDtypeStruct((three, share_rows), bf16),
            jax.ShapeDtypeStruct(traces.shape, f32),
        ),
        in_specs=[pl.BlockSpec(memory_space=pltpu.SMEM)] + [pl.BlockSpec(memory_space=vmem)] * 4,
        out_specs=(pl.BlockSpec(memory_space=vmem), pl.BlockSpec(memory_space=vmem)),
        scratch_shapes=[
            vmem((three, pixels), bf16),
            vmem((three, pixels), bf16),
            vmem((three, side_width), f32),
            vmem((2, width, side_width), f32),
            vmem((5 * width, frames_here), f32),
            vmem((rounds, BLOCK, frames_here), f32),
            vmem((rounds, 4, BLOCK, frames_here), f32),
            vmem((three, frames_here), bf16),
            vmem((three, three), f32),
            vmem((others, three, three), f32),
            vmem((pieces, three, rows_each), f32),
            vmem((others, pieces, three, rows_each), bf16),
            vmem((others, pieces, three, rows_each), bf16),
            dma((4,)), dma((4,)), dma((2,)), dma((2,)),
            dma((rounds, 4)), dma((rounds, 4)), dma((2,)), dma((2,)),
            dma((others,)), dma((others,)), dma((others, pieces)), dma((others, pieces)),
        ],
        compiler_params=pltpu.CompilerParams(
            collective_id=0, has_side_effects=True, vmem_limit_bytes=48 * 1024 * 1024
        ),
    )(block_order.T, frames, footprints.T, support.T, traces)
    return refined.T, updated


def solution(mesh):
    in_specs = (P("pix", "frm"), P("pix", None), P("pix", None), P("pix", "frm"), P())
    out_specs = (P(("pix", "frm"), None), P("pix", "frm"))
    body = functools.partial(shards, mesh.shape["pix"], mesh.shape["frm"])
    return jax.shard_map(body, mesh=mesh, in_specs=in_specs, out_specs=out_specs, check_vma=False)
```

```python
import functools

import jax
import jax.numpy as jnp
from jax import lax
from jax.experimental import pallas as pl
from jax.experimental.pallas import tpu as pltpu
from jax.sharding import PartitionSpec as P

BLOCK = 32
TILE = 16
MESH = pl.DeviceIdType.MESH
OFFSETS = (-2, -1, 1, 2)
WHOLE = 4
f32, bf16 = jnp.float32, jnp.bfloat16


def dot(a, b, dims=((1,), (0,))):
    return lax.dot_general(a, b, (dims, ((), ())), preferred_element_type=f32)


def halves(x):
    high = x.astype(bf16)
    return high, (x - high.astype(f32)).astype(bf16)


def kernel(
    owners, shares, order_hbm, frames_hbm, foot_hbm, support_hbm, traces_hbm, refined_ref, updated_ref,
    order_ref, frames_ref, support_ref, act, keep, near_traces, drive, corr, side_drive, side_corr, change,
    blk_out, blk_in, near, near_far, frames_in, part_own, part_out, part_in,
    in_sem, order_sem, a_send, a_recv, b_send, b_recv, k_send, k_recv, c_send, c_recv, d_send, d_recv,
    x_send, x_recv, y_send, y_recv, e_send, e_recv, f_send, f_recv,
):
    slab, mine = lax.axis_index("pix"), lax.axis_index("frm")
    pixels, frames_here = frames_ref.shape
    three = act.shape[0]
    width = three // 3
    sweeps = width // BLOCK
    share_rows = pixels // shares
    whole_pieces, rows_each = frames_in.shape[1], frames_in.shape[2]
    part_pieces = share_rows // rows_each - whole_pieces
    barrier = pltpu.get_barrier_semaphore()

    def present(offset):
        return slab + offset >= 0 if offset < 0 else slab + offset < owners

    def slot(offset):
        return OFFSETS.index(offset)

    def partner(d):
        return lax.rem(mine + d, shares)

    for offset in OFFSETS:
        @pl.when(present(offset))
        def _():
            pl.semaphore_signal(barrier, inc=1, device_id=(slab + offset, mine), device_id_type=MESH)
    for d in range(1, shares):
        pl.semaphore_signal(barrier, inc=1, device_id=(slab, partner(d)), device_id_type=MESH)

    groups = in_sem.shape[0] - 1
    chunk = pixels // groups

    def bring(c):
        rows = pl.ds(c * chunk, chunk)
        return [pltpu.make_async_copy(foot_hbm.at[:, rows], act.at[:, rows], in_sem.at[c, 0]),
                pltpu.make_async_copy(frames_hbm.at[rows], frames_ref.at[rows], in_sem.at[c, 1])]

    fetch_support = pltpu.make_async_copy(support_hbm, support_ref, in_sem.at[groups, 0])
    fetch_traces = pltpu.make_async_copy(traces_hbm, near_traces.at[pl.ds(width, width)], in_sem.at[groups, 1])
    fetch_order = pltpu.make_async_copy(order_hbm, order_ref, order_sem)
    fetch_support.start()
    for c in range(groups):
        for copy in bring(c):
            copy.start()
        if c == 0:
            fetch_traces.start()
            fetch_order.start()

    for offset in OFFSETS:
        @pl.when(jnp.logical_not(present(offset)))
        def _():
            for step in range(sweeps - 1):
                blk_in[step, slot(offset)] = jnp.zeros((BLOCK, frames_here), f32)
            if abs(offset) == 1:
                at = 0 if offset < 0 else 1
                side_drive[at] = jnp.zeros(side_drive.shape[1:], f32)
                side_corr[at] = jnp.zeros(side_corr.shape[1:], f32)
                row = (1 + offset) * width
                near_traces[row : row + width, :] = jnp.zeros((width, frames_here), f32)
                near[row : row + width, :] = jnp.zeros((width, frames_here), bf16)
                for d in range(1, shares):
                    near_far[d - 1, row : row + width, :] = jnp.zeros((width, frames_here), bf16)

    peers = jnp.minimum(slab, 2) + jnp.minimum(owners - 1 - slab, 2) + shares - 1
    pl.semaphore_wait(barrier, peers)

    def remote(src, dst, send, recv, to):
        return pltpu.make_async_remote_copy(
            src_ref=src, dst_ref=dst, send_sem=send, recv_sem=recv, device_id=to, device_id_type=MESH)

    def side_of(offset):
        return 1 if offset < 0 else 0

    def rows_for(offset):
        return pl.ds(0 if offset < 0 else 2 * width, width)

    def rows_there(offset):
        return pl.ds((1 - offset) * width, width)

    def send_traces(offset):
        at = side_of(offset)
        return remote(traces_hbm, near_traces.at[rows_there(offset)], a_send.at[at], a_recv.at[at], (slab + offset, mine))

    def send_drive(offset):
        at = side_of(offset)
        return remote(drive.at[rows_for(offset)], side_drive.at[at], b_send.at[at], b_recv.at[at], (slab + offset, mine))

    def send_corr(offset):
        at = side_of(offset)
        return remote(corr.at[rows_for(offset)], side_corr.at[at], k_send.at[at], k_recv.at[at], (slab + offset, mine))

    def send_block(step, offset):
        k = slot(-offset)
        return remote(blk_out.at[step], blk_in.at[step, k], c_send.at[step, k], c_recv.at[step, k], (slab + offset, mine))

    own_rows = pl.ds(width, width)

    def send_near(offset):
        at = side_of(offset)
        return remote(near.at[own_rows], near.at[rows_there(offset)], d_send.at[at], d_recv.at[at], (slab + offset, mine))

    def send_far(d):
        return remote(near.at[own_rows], near_far.at[d - 1, own_rows], x_send.at[d - 1], x_recv.at[d - 1], (slab, partner(d)))

    def relay(d, offset):
        at = side_of(offset)
        return remote(near_far.at[d - 1, own_rows], near_far.at[d - 1, rows_there(offset)],
                      y_send.at[d - 1, at], y_recv.at[d - 1, at], (slab + offset, mine))

    def first_of(who, piece):
        return pl.multiple_of(who * share_rows + piece * rows_each, rows_each)

    def send_frames(d, piece):
        return remote(frames_hbm.at[pl.ds(first_of(partner(d), piece), rows_each)], frames_in.at[d - 1, piece],
                      e_send.at[d - 1, piece], e_recv.at[d - 1, piece], (slab, partner(d)))

    def send_part(d, piece):
        return remote(part_out.at[d - 1, piece], part_in.at[d - 1, piece],
                      f_send.at[d - 1, piece], f_recv.at[d - 1, piece], (slab, partner(d)))

    def start(copy, offset):
        @pl.when(present(offset))
        def _():
            copy(offset).start()

    def arrive(copy, offset):
        @pl.when(present(-offset))
        def _():
            copy(offset).wait_recv()

    def left(copy, offset):
        @pl.when(present(offset))
        def _():
            copy(offset).wait_send()

    for offset in (-1, 1):
        start(send_traces, offset)
    for piece in range(whole_pieces):
        for d in range(1, shares):
            send_frames(d, piece).start()

    line = lax.broadcasted_iota(jnp.int32, (three, 1), 0)
    window_of = line // width
    usable = jnp.where(
        window_of == 0, (slab > 0).astype(f32), jnp.where(window_of == 2, (slab < owners - 1).astype(f32), 1.0))
    fetch_support.wait()
    supported = (support_ref[...].astype(f32) * usable).astype(bf16)
    tiles = support_ref.shape[1]
    tile_of = lax.broadcasted_iota(jnp.int32, (tiles, chunk), 1) // TILE
    tile_is = lax.broadcasted_iota(jnp.int32, (tiles, chunk), 0)
    for c in range(groups):
        rows = slice(c * chunk, (c + 1) * chunk)
        spread = (tile_is == tile_of + c * (chunk // TILE)).astype(f32).astype(bf16)
        mask = dot(supported, spread).astype(bf16)
        keep[:, rows] = mask
        from_foot, from_frames = bring(c)
        from_foot.wait()
        active = act[:, rows] * mask
        act[:, rows] = active
        together = dot(active, active, ((1,), (1,)))
        corr[...] = together if c == 0 else corr[...] + together
        from_frames.wait()
        loads = dot(active, frames_ref[rows, :])
        drive[...] = loads if c == 0 else drive[...] + loads

    for offset in (-1, 1):
        start(send_corr, offset)
    corr_high, corr_low = halves(corr[...])
    fetch_traces.wait()
    for offset in (-1, 1):
        arrive(send_traces, offset)
    high, low = halves(near_traces[...])
    both = dot(jnp.concatenate([corr_high, corr_low], axis=0), high)
    drive[...] -= both[:three] + both[three:] + dot(corr_high, low)
    for offset in (-1, 1):
        start(send_drive, offset)
    fetch_order.wait()
    for offset in (-1, 1):
        arrive(send_corr, offset)
    parts = [side_corr[0], corr[width : 2 * width, :], side_corr[1]]
    row = lax.broadcasted_iota(jnp.int32, (width, three), 0)
    column = lax.broadcasted_iota(jnp.int32, (width, three), 1)
    diagonal = jnp.zeros((width, 1), f32)
    stacked, tops = [], []
    for i, part in enumerate(parts):
        diagonal += jnp.sum(jnp.where(column == row + (2 - i) * width, part, 0.0), axis=1, keepdims=True)
        high, low = halves(part)
        tops.append(high)
        stacked.append(jnp.concatenate([high, low], axis=0))
    block_of = lax.broadcasted_iota(jnp.int32, (width, 1), 0) // BLOCK
    for offset in (-1, 1):
        arrive(send_drive, offset)
    current = near_traces[width : 2 * width, :]
    wanted = drive[width : 2 * width, :] + side_drive[0] + side_drive[1]
    rate = 1.0 / (diagonal + 1.0)

    for step in range(sweeps):
        picked = order_ref[step, slab]
        after = jnp.where(block_of == picked, jnp.maximum(current + wanted * rate, 0.0), current)
        if step < sweeps - 1:
            moved = after - current
            block = jnp.zeros((BLOCK, frames_here), f32)
            for k in range(sweeps):
                block = jnp.where(picked == k, moved[k * BLOCK : (k + 1) * BLOCK], block)
            blk_out[step] = block
            for offset in OFFSETS:
                start(functools.partial(send_block, step), offset)
            change[2 * width : 3 * width, :] = moved
            for offset in OFFSETS:
                arrive(functools.partial(send_block, step), offset)
            for offset in OFFSETS:
                there = jnp.clip(slab + offset, 0, owners - 1)
                first = (2 + offset) * width
                news = jnp.concatenate([blk_in[step, slot(offset)]] * sweeps, axis=0)
                change[first : first + width, :] = jnp.where(block_of == order_ref[step, there], news, 0.0)
            high, low = halves(change[...])
            for i in range(3):
                span = slice(i * width, i * width + three)
                both = dot(stacked[i], high[span])
                wanted -= both[:width] + both[width:] + dot(tops[i], low[span])
        current = after
    near[width : 2 * width, :] = current.astype(bf16)
    for offset in (-1, 1):
        start(send_near, offset)
    for d in range(1, shares):
        send_far(d).start()
    updated_ref[...] = current

    for offset in (-1, 1):
        arrive(send_near, offset)
    traces_near = near[...]
    over_frames = ((1,), (1,))
    gram_here = dot(traces_near, traces_near, over_frames)
    both_here = jnp.concatenate(halves(gram_here), axis=0)

    def residual(first):
        rows = pl.ds(first, rows_each)
        fitted = dot(both_here, act[:, rows])
        return dot(traces_near, frames_ref[rows, :], over_frames) - fitted[:three] - fitted[three:]

    for piece in range(part_pieces):
        for d in range(1, shares):
            part_out[d - 1, piece] = residual(first_of(partner(d), whole_pieces + piece)).astype(bf16)
            send_part(d, piece).start()
        if piece == 0:
            for d in range(1, shares):
                send_far(d).wait_recv()
                for offset in (-1, 1):
                    start(functools.partial(relay, d), offset)
    for piece in range(part_pieces):
        part_own[piece] = residual(first_of(mine, whole_pieces + piece))

    gram = gram_here
    for d in range(1, shares):
        for offset in (-1, 1):
            arrive(functools.partial(relay, d), offset)
        gram += dot(near_far[d - 1], near_far[d - 1], over_frames)
    grow = lax.broadcasted_iota(jnp.int32, (three, three), 0)
    gcol = lax.broadcasted_iota(jnp.int32, (three, three), 1)
    rate = 1.0 / (jnp.sum(jnp.where(grow == gcol, gram, 0.0), axis=1, keepdims=True) + 1.0)
    gram_high, gram_low = halves(gram)
    gram_both = jnp.concatenate([gram_high, gram_low], axis=0)
    line_block = lax.rem(line, width) // BLOCK
    picks = []
    for step in range(sweeps):
        chosen = [order_ref[step, jnp.clip(slab - 1 + w, 0, owners - 1)] for w in range(3)]
        chosen = jnp.where(window_of == 0, chosen[0], jnp.where(window_of == 1, chosen[1], chosen[2]))
        picks.append(line_block == chosen)

    def refine(piece, left_over):
        here = pl.ds(first_of(mine, piece), rows_each)
        shaped = act[:, here].astype(f32)
        mask = keep[:, here].astype(f32)
        for step in range(sweeps):
            after = jnp.where(picks[step], jnp.maximum(shaped + left_over * rate, 0.0) * mask, shaped)
            if step < sweeps - 1:
                moved, rest = halves(after - shaped)
                lost = dot(gram_both, moved)
                left_over = left_over - (lost[:three] + lost[three:] + dot(gram_high, rest))
            shaped = after
        refined_ref[:, piece * rows_each : (piece + 1) * rows_each] = shaped.astype(bf16)

    for piece in range(whole_pieces):
        here = pl.ds(first_of(mine, piece), rows_each)
        fitted = dot(gram_both, act[:, here])
        left_over = dot(traces_near, frames_ref[here, :], over_frames) - fitted[:three] - fitted[three:]
        for d in range(1, shares):
            send_frames(d, piece).wait_recv()
            left_over += dot(near_far[d - 1], frames_in[d - 1, piece], over_frames)
        refine(piece, left_over)
    for piece in range(part_pieces):
        left_over = part_own[piece]
        for d in range(1, shares):
            send_part(d, piece).wait_recv()
            left_over += part_in[d - 1, piece].astype(f32)
        refine(whole_pieces + piece, left_over)

    for offset in OFFSETS:
        for step in range(sweeps - 1):
            left(functools.partial(send_block, step), offset)
    for offset in (-1, 1):
        for copy in (send_traces, send_drive, send_corr, send_near):
            left(copy, offset)
        for d in range(1, shares):
            left(functools.partial(relay, d), offset)
    for d in range(1, shares):
        send_far(d).wait_send()
        for piece in range(whole_pieces):
            send_frames(d, piece).wait_send()
        for piece in range(part_pieces):
            send_part(d, piece).wait_send()


def shards(owners, shares, frames, footprints, support, traces, block_order):
    pixels, frames_here = frames.shape
    width = traces.shape[0]
    three = 3 * width
    rounds = max(width // BLOCK - 1, 1)
    share_rows = pixels // shares
    rows_each = min(share_rows // 2, 256)
    pieces = share_rows // rows_each
    whole_pieces = pieces * WHOLE // 8
    part_pieces = pieces - whole_pieces
    others = max(shares - 1, 1)
    groups = 4
    vmem, dma = pltpu.VMEM, pltpu.SemaphoreType.DMA
    refined, updated = pl.pallas_call(
        functools.partial(kernel, owners, shares),
        out_shape=(
            jax.ShapeDtypeStruct((three, share_rows), bf16),
            jax.ShapeDtypeStruct(traces.shape, f32),
        ),
        in_specs=[pl.BlockSpec(memory_space=pl.ANY)] * 5,
        out_specs=(pl.BlockSpec(memory_space=vmem), pl.BlockSpec(memory_space=vmem)),
        scratch_shapes=[
            pltpu.SMEM(block_order.shape[::-1], jnp.int32),
            vmem(frames.shape, bf16),
            vmem(support.shape[::-1], jnp.int32),
            vmem((three, pixels), bf16),
            vmem((three, pixels), bf16),
            vmem((three, frames_here), f32),
            vmem((three, frames_here), f32),
            vmem((three, three), f32),
            vmem((2, width, frames_here), f32),
            vmem((2, width, three), f32),
            vmem((5 * width, frames_here), f32),
            vmem((rounds, BLOCK, frames_here), f32),
            vmem((rounds, 4, BLOCK, frames_here), f32),
            vmem((three, frames_here), bf16),
            vmem((others, three, frames_here), bf16),
            vmem((others, whole_pieces, rows_each, frames_here), bf16),
            vmem((part_pieces, three, rows_each), f32),
            vmem((others, part_pieces, three, rows_each), bf16),
            vmem((others, part_pieces, three, rows_each), bf16),
            dma((groups + 1, 2)), dma,
            dma((2,)), dma((2,)), dma((2,)), dma((2,)), dma((2,)), dma((2,)),
            dma((rounds, 4)), dma((rounds, 4)), dma((2,)), dma((2,)),
            dma((others,)), dma((others,)), dma((others, 2)), dma((others, 2)),
            dma((others, whole_pieces)), dma((others, whole_pieces)),
            dma((others, part_pieces)), dma((others, part_pieces)),
        ],
        compiler_params=pltpu.CompilerParams(
            collective_id=0, has_side_effects=True, vmem_limit_bytes=56 * 1024 * 1024
        ),
    )(block_order.T, frames, footprints.T, support.T, traces)
    return refined.T, updated


def solution(mesh):
    in_specs = (P("pix", "frm"), P("pix", None), P("pix", None), P("pix", "frm"), P())
    out_specs = (P(("pix", "frm"), None), P("pix", "frm"))
    body = functools.partial(shards, mesh.shape["pix"], mesh.shape["frm"])
    return jax.shard_map(body, mesh=mesh, in_specs=in_specs, out_specs=out_specs, check_vma=False)
```

```python
import functools

import jax
import jax.numpy as jnp
from jax import lax
from jax.experimental import pallas as pl
from jax.experimental.pallas import tpu as pltpu
from jax.sharding import PartitionSpec as P

BLOCK = 32
TILE = 16
MESH = pl.DeviceIdType.MESH
OFFSETS = (-2, -1, 1, 2)
WHOLE = 4
f32, bf16 = jnp.float32, jnp.bfloat16


def dot(a, b, dims=((1,), (0,))):
    return lax.dot_general(a, b, (dims, ((), ())), preferred_element_type=f32)


def halves(x):
    high = x.astype(bf16)
    return high, (x - high.astype(f32)).astype(bf16)


def kernel(
    owners, shares, order_hbm, frames_hbm, foot_hbm, support_hbm, traces_hbm, refined_hbm, updated_hbm,
    order_ref, frames_ref, support_ref, act, keep, near_traces, drive, corr, side_drive, side_corr, change,
    blk_out, blk_in, near, near_far, frames_in, part_own, part_out, part_in,
    refined_ref, updated_ref, out_sem, in_sem, order_sem, a_send, a_recv, b_send, b_recv, k_send, k_recv, c_send, c_recv, d_send, d_recv,
    x_send, x_recv, y_send, y_recv, e_send, e_recv, f_send, f_recv,
):
    slab, mine = lax.axis_index("pix"), lax.axis_index("frm")
    pixels, frames_here = frames_ref.shape
    three = act.shape[0]
    width = three // 3
    sweeps = width // BLOCK
    share_rows = pixels // shares
    whole_pieces, rows_each = frames_in.shape[1], frames_in.shape[2]
    part_pieces = share_rows // rows_each - whole_pieces
    barrier = pltpu.get_barrier_semaphore()

    def present(offset):
        return slab + offset >= 0 if offset < 0 else slab + offset < owners

    def slot(offset):
        return OFFSETS.index(offset)

    def partner(d):
        return lax.rem(mine + d, shares)

    for offset in OFFSETS:
        @pl.when(present(offset))
        def _():
            pl.semaphore_signal(barrier, inc=1, device_id=(slab + offset, mine), device_id_type=MESH)
    for d in range(1, shares):
        pl.semaphore_signal(barrier, inc=1, device_id=(slab, partner(d)), device_id_type=MESH)

    groups = in_sem.shape[0] - 1
    chunk = pixels // groups

    def bring(c):
        rows = pl.ds(c * chunk, chunk)
        return [pltpu.make_async_copy(foot_hbm.at[:, rows], act.at[:, rows], in_sem.at[c, 0]),
                pltpu.make_async_copy(frames_hbm.at[rows], frames_ref.at[rows], in_sem.at[c, 1])]

    fetch_support = pltpu.make_async_copy(support_hbm, support_ref, in_sem.at[groups, 0])
    fetch_traces = pltpu.make_async_copy(traces_hbm, near_traces.at[pl.ds(width, width)], in_sem.at[groups, 1])
    fetch_order = pltpu.make_async_copy(order_hbm, order_ref, order_sem)
    fetch_support.start()
    for c in range(groups):
        for copy in bring(c):
            copy.start()
        if c == 0:
            fetch_traces.start()
            fetch_order.start()

    for offset in OFFSETS:
        @pl.when(jnp.logical_not(present(offset)))
        def _():
            for step in range(sweeps - 1):
                blk_in[step, slot(offset)] = jnp.zeros((BLOCK, frames_here), f32)
            if abs(offset) == 1:
                at = 0 if offset < 0 else 1
                side_drive[at] = jnp.zeros(side_drive.shape[1:], f32)
                side_corr[at] = jnp.zeros(side_corr.shape[1:], f32)
                row = (1 + offset) * width
                near_traces[row : row + width, :] = jnp.zeros((width, frames_here), f32)
                near[row : row + width, :] = jnp.zeros((width, frames_here), bf16)
                for d in range(1, shares):
                    near_far[d - 1, row : row + width, :] = jnp.zeros((width, frames_here), bf16)

    peers = jnp.minimum(slab, 2) + jnp.minimum(owners - 1 - slab, 2) + shares - 1
    pl.semaphore_wait(barrier, peers)

    def remote(src, dst, send, recv, to):
        return pltpu.make_async_remote_copy(
            src_ref=src, dst_ref=dst, send_sem=send, recv_sem=recv, device_id=to, device_id_type=MESH)

    def side_of(offset):
        return 1 if offset < 0 else 0

    def rows_for(offset):
        return pl.ds(0 if offset < 0 else 2 * width, width)

    def rows_there(offset):
        return pl.ds((1 - offset) * width, width)

    def send_traces(offset):
        at = side_of(offset)
        return remote(traces_hbm, near_traces.at[rows_there(offset)], a_send.at[at], a_recv.at[at], (slab + offset, mine))

    def send_drive(offset):
        at = side_of(offset)
        return remote(drive.at[rows_for(offset)], side_drive.at[at], b_send.at[at], b_recv.at[at], (slab + offset, mine))

    def send_corr(offset):
        at = side_of(offset)
        return remote(corr.at[rows_for(offset)], side_corr.at[at], k_send.at[at], k_recv.at[at], (slab + offset, mine))

    def send_block(step, offset):
        k = slot(-offset)
        return remote(blk_out.at[step], blk_in.at[step, k], c_send.at[step, k], c_recv.at[step, k], (slab + offset, mine))

    own_rows = pl.ds(width, width)

    def send_near(offset):
        at = side_of(offset)
        return remote(near.at[own_rows], near.at[rows_there(offset)], d_send.at[at], d_recv.at[at], (slab + offset, mine))

    def send_far(d):
        return remote(near.at[own_rows], near_far.at[d - 1, own_rows], x_send.at[d - 1], x_recv.at[d - 1], (slab, partner(d)))

    def relay(d, offset):
        at = side_of(offset)
        return remote(near_far.at[d - 1, own_rows], near_far.at[d - 1, rows_there(offset)],
                      y_send.at[d - 1, at], y_recv.at[d - 1, at], (slab + offset, mine))

    def first_of(who, piece):
        return pl.multiple_of(who * share_rows + piece * rows_each, rows_each)

    def send_frames(d, piece):
        return remote(frames_hbm.at[pl.ds(first_of(partner(d), piece), rows_each)], frames_in.at[d - 1, piece],
                      e_send.at[d - 1, piece], e_recv.at[d - 1, piece], (slab, partner(d)))

    def send_part(d, piece):
        return remote(part_out.at[d - 1, piece], part_in.at[d - 1, piece],
                      f_send.at[d - 1, piece], f_recv.at[d - 1, piece], (slab, partner(d)))

    def start(copy, offset):
        @pl.when(present(offset))
        def _():
            copy(offset).start()

    def arrive(copy, offset):
        @pl.when(present(-offset))
        def _():
            copy(offset).wait_recv()

    def left(copy, offset):
        @pl.when(present(offset))
        def _():
            copy(offset).wait_send()

    for offset in (-1, 1):
        start(send_traces, offset)
    for piece in range(whole_pieces):
        for d in range(1, shares):
            send_frames(d, piece).start()

    line = lax.broadcasted_iota(jnp.int32, (three, 1), 0)
    window_of = line // width
    usable = jnp.where(
        window_of == 0, (slab > 0).astype(f32), jnp.where(window_of == 2, (slab < owners - 1).astype(f32), 1.0))
    fetch_support.wait()
    supported = (support_ref[...].astype(f32) * usable).astype(bf16)
    tiles = support_ref.shape[1]
    tile_of = lax.broadcasted_iota(jnp.int32, (tiles, chunk), 1) // TILE
    tile_is = lax.broadcasted_iota(jnp.int32, (tiles, chunk), 0)
    for c in range(groups):
        rows = slice(c * chunk, (c + 1) * chunk)
        spread = (tile_is == tile_of + c * (chunk // TILE)).astype(f32).astype(bf16)
        mask = dot(supported, spread).astype(bf16)
        keep[:, rows] = mask
        from_foot, from_frames = bring(c)
        from_foot.wait()
        active = act[:, rows] * mask
        act[:, rows] = active
        together = dot(active, active, ((1,), (1,)))
        corr[...] = together if c == 0 else corr[...] + together
        from_frames.wait()
        loads = dot(active, frames_ref[rows, :])
        drive[...] = loads if c == 0 else drive[...] + loads

    for offset in (-1, 1):
        start(send_corr, offset)
    corr_high, corr_low = halves(corr[...])
    fetch_traces.wait()
    for offset in (-1, 1):
        arrive(send_traces, offset)
    high, low = halves(near_traces[...])
    both = dot(jnp.concatenate([corr_high, corr_low], axis=0), high)
    drive[...] -= both[:three] + both[three:] + dot(corr_high, low)
    for offset in (-1, 1):
        start(send_drive, offset)
    fetch_order.wait()
    for offset in (-1, 1):
        arrive(send_corr, offset)
    parts = [side_corr[0], corr[width : 2 * width, :], side_corr[1]]
    row = lax.broadcasted_iota(jnp.int32, (width, three), 0)
    column = lax.broadcasted_iota(jnp.int32, (width, three), 1)
    diagonal = jnp.zeros((width, 1), f32)
    stacked, tops = [], []
    for i, part in enumerate(parts):
        diagonal += jnp.sum(jnp.where(column == row + (2 - i) * width, part, 0.0), axis=1, keepdims=True)
        high, low = halves(part)
        tops.append(high)
        stacked.append(jnp.concatenate([high, low], axis=0))
    block_of = lax.broadcasted_iota(jnp.int32, (width, 1), 0) // BLOCK
    for offset in (-1, 1):
        arrive(send_drive, offset)
    current = near_traces[width : 2 * width, :]
    wanted = drive[width : 2 * width, :] + side_drive[0] + side_drive[1]
    rate = 1.0 / (diagonal + 1.0)

    for step in range(sweeps):
        picked = order_ref[step, slab]
        after = jnp.where(block_of == picked, jnp.maximum(current + wanted * rate, 0.0), current)
        if step < sweeps - 1:
            moved = after - current
            block = jnp.zeros((BLOCK, frames_here), f32)
            for k in range(sweeps):
                block = jnp.where(picked == k, moved[k * BLOCK : (k + 1) * BLOCK], block)
            blk_out[step] = block
            for offset in OFFSETS:
                start(functools.partial(send_block, step), offset)
            change[2 * width : 3 * width, :] = moved
            for offset in OFFSETS:
                arrive(functools.partial(send_block, step), offset)
            for offset in OFFSETS:
                there = jnp.clip(slab + offset, 0, owners - 1)
                first = (2 + offset) * width
                news = jnp.concatenate([blk_in[step, slot(offset)]] * sweeps, axis=0)
                change[first : first + width, :] = jnp.where(block_of == order_ref[step, there], news, 0.0)
            high, low = halves(change[...])
            for i in range(3):
                span = slice(i * width, i * width + three)
                both = dot(stacked[i], high[span])
                wanted -= both[:width] + both[width:] + dot(tops[i], low[span])
        current = after
    near[width : 2 * width, :] = current.astype(bf16)
    for offset in (-1, 1):
        start(send_near, offset)
    for d in range(1, shares):
        send_far(d).start()
    updated_ref[...] = current
    pltpu.make_async_copy(updated_ref, updated_hbm, out_sem.at[whole_pieces + part_pieces]).start()

    for offset in (-1, 1):
        arrive(send_near, offset)
    traces_near = near[...]
    over_frames = ((1,), (1,))
    gram_here = dot(traces_near, traces_near, over_frames)
    both_here = jnp.concatenate(halves(gram_here), axis=0)

    def residual(first):
        rows = pl.ds(first, rows_each)
        fitted = dot(both_here, act[:, rows])
        return dot(traces_near, frames_ref[rows, :], over_frames) - fitted[:three] - fitted[three:]

    for piece in range(part_pieces):
        for d in range(1, shares):
            part_out[d - 1, piece] = residual(first_of(partner(d), whole_pieces + piece)).astype(bf16)
            send_part(d, piece).start()
        if piece == 0:
            for d in range(1, shares):
                send_far(d).wait_recv()
                for offset in (-1, 1):
                    start(functools.partial(relay, d), offset)
    for piece in range(part_pieces):
        part_own[piece] = residual(first_of(mine, whole_pieces + piece))

    gram = gram_here
    for d in range(1, shares):
        for offset in (-1, 1):
            arrive(functools.partial(relay, d), offset)
        gram += dot(near_far[d - 1], near_far[d - 1], over_frames)
    grow = lax.broadcasted_iota(jnp.int32, (three, three), 0)
    gcol = lax.broadcasted_iota(jnp.int32, (three, three), 1)
    rate = 1.0 / (jnp.sum(jnp.where(grow == gcol, gram, 0.0), axis=1, keepdims=True) + 1.0)
    gram_high, gram_low = halves(gram)
    gram_both = jnp.concatenate([gram_high, gram_low], axis=0)
    line_block = lax.rem(line, width) // BLOCK
    picks = []
    for step in range(sweeps):
        chosen = [order_ref[step, jnp.clip(slab - 1 + w, 0, owners - 1)] for w in range(3)]
        chosen = jnp.where(window_of == 0, chosen[0], jnp.where(window_of == 1, chosen[1], chosen[2]))
        picks.append(line_block == chosen)

    def deposit(piece):
        span = pl.ds(piece * rows_each, rows_each)
        return pltpu.make_async_copy(refined_ref.at[:, span], refined_hbm.at[:, span], out_sem.at[piece])

    def refine(piece, left_over):
        here = pl.ds(first_of(mine, piece), rows_each)
        shaped = act[:, here].astype(f32)
        mask = keep[:, here].astype(f32)
        for step in range(sweeps):
            after = jnp.where(picks[step], jnp.maximum(shaped + left_over * rate, 0.0) * mask, shaped)
            if step < sweeps - 1:
                moved, rest = halves(after - shaped)
                lost = dot(gram_both, moved)
                left_over = left_over - (lost[:three] + lost[three:] + dot(gram_high, rest))
            shaped = after
        refined_ref[:, piece * rows_each : (piece + 1) * rows_each] = shaped.astype(bf16)
        deposit(piece).start()

    for piece in range(whole_pieces):
        here = pl.ds(first_of(mine, piece), rows_each)
        fitted = dot(gram_both, act[:, here])
        left_over = dot(traces_near, frames_ref[here, :], over_frames) - fitted[:three] - fitted[three:]
        for d in range(1, shares):
            send_frames(d, piece).wait_recv()
            left_over += dot(near_far[d - 1], frames_in[d - 1, piece], over_frames)
        refine(piece, left_over)
    for piece in range(part_pieces):
        left_over = part_own[piece]
        for d in range(1, shares):
            send_part(d, piece).wait_recv()
            left_over += part_in[d - 1, piece].astype(f32)
        refine(whole_pieces + piece, left_over)

    for piece in range(whole_pieces + part_pieces):
        deposit(piece).wait()
    pltpu.make_async_copy(updated_ref, updated_hbm, out_sem.at[whole_pieces + part_pieces]).wait()
    for offset in OFFSETS:
        for step in range(sweeps - 1):
            left(functools.partial(send_block, step), offset)
    for offset in (-1, 1):
        for copy in (send_traces, send_drive, send_corr, send_near):
            left(copy, offset)
        for d in range(1, shares):
            left(functools.partial(relay, d), offset)
    for d in range(1, shares):
        send_far(d).wait_send()
        for piece in range(whole_pieces):
            send_frames(d, piece).wait_send()
        for piece in range(part_pieces):
            send_part(d, piece).wait_send()


def deliver_kernel(refined_ref, updated_ref, refined_out, updated_out, refined_held, updated_held, sem):
    rows = refined_ref.shape[0] // 4
    moves = [(updated_ref, updated_held, updated_out)]
    for i in range(4):
        part = pl.ds(i * rows, rows)
        moves.append((refined_ref.at[part], refined_held.at[part], refined_out.at[part]))
    inward = [pltpu.make_async_copy(a, b, sem.at[0, i]) for i, (a, b, c) in enumerate(moves)]
    outward = [pltpu.make_async_copy(b, c, sem.at[1, i]) for i, (a, b, c) in enumerate(moves)]
    for copy in inward:
        copy.start()
    for copy, onward in zip(inward, outward):
        copy.wait()
        onward.start()
    for copy in outward:
        copy.wait()


def deliver(refined, updated):
    like = [jax.ShapeDtypeStruct(x.shape, x.dtype) for x in (refined, updated)]
    anywhere = pl.BlockSpec(memory_space=pl.ANY)
    refined, updated = pl.pallas_call(
        deliver_kernel, out_shape=like, in_specs=[anywhere] * 2, out_specs=[anywhere] * 2,
        scratch_shapes=[pltpu.VMEM(x.shape, x.dtype) for x in like] + [pltpu.SemaphoreType.DMA((2, 5))],
        compiler_params=pltpu.CompilerParams(vmem_limit_bytes=56 * 1024 * 1024),
    )(refined, updated)
    return refined.T, updated


def shards(owners, shares, frames, footprints, support, traces, block_order):
    pixels, frames_here = frames.shape
    width = traces.shape[0]
    three = 3 * width
    rounds = max(width // BLOCK - 1, 1)
    share_rows = pixels // shares
    rows_each = min(share_rows // 2, 256)
    pieces = share_rows // rows_each
    whole_pieces = pieces * WHOLE // 8
    part_pieces = pieces - whole_pieces
    others = max(shares - 1, 1)
    groups = 4
    vmem, dma = pltpu.VMEM, pltpu.SemaphoreType.DMA
    refined, updated = pl.pallas_call(
        functools.partial(kernel, owners, shares),
        out_shape=(
            jax.ShapeDtypeStruct((three, share_rows), bf16),
            jax.ShapeDtypeStruct(traces.shape, f32),
        ),
        in_specs=[pl.BlockSpec(memory_space=pl.ANY)] * 5,
        out_specs=(pl.BlockSpec(memory_space=pl.ANY), pl.BlockSpec(memory_space=pl.ANY)),
        scratch_shapes=[
            pltpu.SMEM(block_order.shape[::-1], jnp.int32),
            vmem(frames.shape, bf16),
            vmem(support.shape[::-1], jnp.int32),
            vmem((three, pixels), bf16),
            vmem((three, pixels), bf16),
            vmem((three, frames_here), f32),
            vmem((three, frames_here), f32),
            vmem((three, three), f32),
            vmem((2, width, frames_here), f32),
            vmem((2, width, three), f32),
            vmem((5 * width, frames_here), f32),
            vmem((rounds, BLOCK, frames_here), f32),
            vmem((rounds, 4, BLOCK, frames_here), f32),
            vmem((three, frames_here), bf16),
            vmem((others, three, frames_here), bf16),
            vmem((others, whole_pieces, rows_each, frames_here), bf16),
            vmem((part_pieces, three, rows_each), f32),
            vmem((others, part_pieces, three, rows_each), bf16),
            vmem((others, part_pieces, three, rows_each), bf16),
            vmem((three, share_rows), bf16), vmem(traces.shape, f32), dma((pieces + 1,)),
            dma((groups + 1, 2)), dma,
            dma((2,)), dma((2,)), dma((2,)), dma((2,)), dma((2,)), dma((2,)),
            dma((rounds, 4)), dma((rounds, 4)), dma((2,)), dma((2,)),
            dma((others,)), dma((others,)), dma((others, 2)), dma((others, 2)),
            dma((others, whole_pieces)), dma((others, whole_pieces)),
            dma((others, part_pieces)), dma((others, part_pieces)),
        ],
        compiler_params=pltpu.CompilerParams(
            collective_id=0, has_side_effects=True, vmem_limit_bytes=56 * 1024 * 1024
        ),
    )(block_order.T, frames, footprints.T, support.T, traces)
    return deliver(refined, updated)


def solution(mesh):
    in_specs = (P("pix", "frm"), P("pix", None), P("pix", None), P("pix", "frm"), P())
    out_specs = (P(("pix", "frm"), None), P("pix", "frm"))
    body = functools.partial(shards, mesh.shape["pix"], mesh.shape["frm"])
    return jax.shard_map(body, mesh=mesh, in_specs=in_specs, out_specs=out_specs, check_vma=False)
```

```python
import functools

import jax
import jax.numpy as jnp
from jax import lax
from jax.experimental import pallas as pl
from jax.experimental.pallas import tpu as pltpu
from jax.sharding import PartitionSpec as P

BLOCK = 32
TILE = 16
MESH = pl.DeviceIdType.MESH
OFFSETS = (-2, -1, 1, 2)
WHOLE = 7
f32, bf16 = jnp.float32, jnp.bfloat16


def dot(a, b, dims=((1,), (0,))):
    return lax.dot_general(a, b, (dims, ((), ())), preferred_element_type=f32)


def halves(x):
    high = x.astype(bf16)
    return high, (x - high.astype(f32)).astype(bf16)


def kernel(
    owners, shares, order_hbm, frames_hbm, foot_hbm, support_hbm, traces_hbm, refined_hbm, updated_hbm,
    order_ref, frames_ref, support_ref, act, keep, near_traces, drive, corr, side_drive, side_corr, change,
    blk_out, blk_in, near, near_far, frames_in, part_own, part_out, part_in,
    refined_ref, updated_ref, out_sem, in_sem, order_sem, a_send, a_recv, b_send, b_recv, k_send, k_recv, c_send, c_recv, d_send, d_recv,
    x_send, x_recv, y_send, y_recv, e_send, e_recv, f_send, f_recv,
):
    slab, mine = lax.axis_index("pix"), lax.axis_index("frm")
    pixels, frames_here = frames_ref.shape
    three = act.shape[0]
    width = three // 3
    sweeps = width // BLOCK
    share_rows = pixels // shares
    whole_pieces, rows_each = frames_in.shape[1], frames_in.shape[2]
    part_pieces = share_rows // rows_each - whole_pieces
    barrier = pltpu.get_barrier_semaphore()

    def present(offset):
        return slab + offset >= 0 if offset < 0 else slab + offset < owners

    def slot(offset):
        return OFFSETS.index(offset)

    def partner(d):
        return lax.rem(mine + d, shares)

    for offset in OFFSETS:
        @pl.when(present(offset))
        def _():
            pl.semaphore_signal(barrier, inc=1, device_id=(slab + offset, mine), device_id_type=MESH)
    for d in range(1, shares):
        pl.semaphore_signal(barrier, inc=1, device_id=(slab, partner(d)), device_id_type=MESH)

    groups = in_sem.shape[0] - 1
    chunk = pixels // groups

    def bring(c):
        rows = pl.ds(c * chunk, chunk)
        return [pltpu.make_async_copy(foot_hbm.at[:, rows], act.at[:, rows], in_sem.at[c, 0]),
                pltpu.make_async_copy(frames_hbm.at[rows], frames_ref.at[rows], in_sem.at[c, 1])]

    fetch_support = pltpu.make_async_copy(support_hbm, support_ref, in_sem.at[groups, 0])
    fetch_traces = pltpu.make_async_copy(traces_hbm, near_traces.at[pl.ds(width, width)], in_sem.at[groups, 1])
    fetch_order = pltpu.make_async_copy(order_hbm, order_ref, order_sem)
    fetch_support.start()
    for c in range(groups):
        for copy in bring(c):
            copy.start()
        if c == 0:
            fetch_traces.start()
            fetch_order.start()

    for offset in OFFSETS:
        @pl.when(jnp.logical_not(present(offset)))
        def _():
            for step in range(sweeps - 1):
                blk_in[step, slot(offset)] = jnp.zeros((BLOCK, frames_here), f32)
            if abs(offset) == 1:
                at = 0 if offset < 0 else 1
                side_drive[at] = jnp.zeros(side_drive.shape[1:], f32)
                side_corr[at] = jnp.zeros(side_corr.shape[1:], f32)
                row = (1 + offset) * width
                near_traces[row : row + width, :] = jnp.zeros((width, frames_here), f32)
                near[row : row + width, :] = jnp.zeros((width, frames_here), bf16)
                for d in range(1, shares):
                    near_far[d - 1, row : row + width, :] = jnp.zeros((width, frames_here), bf16)

    peers = jnp.minimum(slab, 2) + jnp.minimum(owners - 1 - slab, 2) + shares - 1
    pl.semaphore_wait(barrier, peers)

    def remote(src, dst, send, recv, to):
        return pltpu.make_async_remote_copy(
            src_ref=src, dst_ref=dst, send_sem=send, recv_sem=recv, device_id=to, device_id_type=MESH)

    def side_of(offset):
        return 1 if offset < 0 else 0

    def rows_for(offset):
        return pl.ds(0 if offset < 0 else 2 * width, width)

    def rows_there(offset):
        return pl.ds((1 - offset) * width, width)

    def send_traces(offset):
        at = side_of(offset)
        return remote(traces_hbm, near_traces.at[rows_there(offset)], a_send.at[at], a_recv.at[at], (slab + offset, mine))

    def send_drive(offset):
        at = side_of(offset)
        return remote(drive.at[rows_for(offset)], side_drive.at[at], b_send.at[at], b_recv.at[at], (slab + offset, mine))

    def send_corr(offset):
        at = side_of(offset)
        return remote(corr.at[rows_for(offset)], side_corr.at[at], k_send.at[at], k_recv.at[at], (slab + offset, mine))

    def send_block(step, offset):
        k = slot(-offset)
        return remote(blk_out.at[step], blk_in.at[step, k], c_send.at[step, k], c_recv.at[step, k], (slab + offset, mine))

    own_rows = pl.ds(width, width)

    def send_near(offset):
        at = side_of(offset)
        return remote(near.at[own_rows], near.at[rows_there(offset)], d_send.at[at], d_recv.at[at], (slab + offset, mine))

    def send_far(d):
        return remote(near.at[own_rows], near_far.at[d - 1, own_rows], x_send.at[d - 1], x_recv.at[d - 1], (slab, partner(d)))

    def relay(d, offset):
        at = side_of(offset)
        return remote(near_far.at[d - 1, own_rows], near_far.at[d - 1, rows_there(offset)],
                      y_send.at[d - 1, at], y_recv.at[d - 1, at], (slab + offset, mine))

    def first_of(who, piece):
        return pl.multiple_of(who * share_rows + piece * rows_each, rows_each)

    def send_frames(d, piece):
        return remote(frames_hbm.at[pl.ds(first_of(partner(d), piece), rows_each)], frames_in.at[d - 1, piece],
                      e_send.at[d - 1, piece], e_recv.at[d - 1, piece], (slab, partner(d)))

    def send_part(d, piece):
        return remote(part_out.at[d - 1, piece], part_in.at[d - 1, piece],
                      f_send.at[d - 1, piece], f_recv.at[d - 1, piece], (slab, partner(d)))

    def start(copy, offset):
        @pl.when(present(offset))
        def _():
            copy(offset).start()

    def arrive(copy, offset):
        @pl.when(present(-offset))
        def _():
            copy(offset).wait_recv()

    def left(copy, offset):
        @pl.when(present(offset))
        def _():
            copy(offset).wait_send()

    for offset in (-1, 1):
        start(send_traces, offset)
    for piece in range(whole_pieces):
        for d in range(1, shares):
            send_frames(d, piece).start()

    line = lax.broadcasted_iota(jnp.int32, (three, 1), 0)
    window_of = line // width
    usable = jnp.where(
        window_of == 0, (slab > 0).astype(f32), jnp.where(window_of == 2, (slab < owners - 1).astype(f32), 1.0))
    fetch_support.wait()
    supported = (support_ref[...].astype(f32) * usable).astype(bf16)
    tiles = support_ref.shape[1]
    tile_of = lax.broadcasted_iota(jnp.int32, (tiles, chunk), 1) // TILE
    tile_is = lax.broadcasted_iota(jnp.int32, (tiles, chunk), 0)
    for c in range(groups):
        rows = slice(c * chunk, (c + 1) * chunk)
        spread = (tile_is == tile_of + c * (chunk // TILE)).astype(f32).astype(bf16)
        mask = dot(supported, spread).astype(bf16)
        keep[:, rows] = mask
        from_foot, from_frames = bring(c)
        from_foot.wait()
        active = act[:, rows] * mask
        act[:, rows] = active
        together = dot(active, active, ((1,), (1,)))
        corr[...] = together if c == 0 else corr[...] + together
        from_frames.wait()
        loads = dot(active, frames_ref[rows, :])
        drive[...] = loads if c == 0 else drive[...] + loads

    for offset in (-1, 1):
        start(send_corr, offset)
    corr_high, corr_low = halves(corr[...])
    fetch_traces.wait()
    for offset in (-1, 1):
        arrive(send_traces, offset)
    high, low = halves(near_traces[...])
    both = dot(jnp.concatenate([corr_high, corr_low], axis=0), high)
    drive[...] -= both[:three] + both[three:] + dot(corr_high, low)
    for offset in (-1, 1):
        start(send_drive, offset)
    fetch_order.wait()
    for offset in (-1, 1):
        arrive(send_corr, offset)
    parts = [side_corr[0], corr[width : 2 * width, :], side_corr[1]]
    row = lax.broadcasted_iota(jnp.int32, (width, three), 0)
    column = lax.broadcasted_iota(jnp.int32, (width, three), 1)
    diagonal = jnp.zeros((width, 1), f32)
    stacked, tops = [], []
    for i, part in enumerate(parts):
        diagonal += jnp.sum(jnp.where(column == row + (2 - i) * width, part, 0.0), axis=1, keepdims=True)
        high, low = halves(part)
        tops.append(high)
        stacked.append(jnp.concatenate([high, low], axis=0))
    block_of = lax.broadcasted_iota(jnp.int32, (width, 1), 0) // BLOCK
    for offset in (-1, 1):
        arrive(send_drive, offset)
    current = near_traces[width : 2 * width, :]
    wanted = drive[width : 2 * width, :] + side_drive[0] + side_drive[1]
    rate = 1.0 / (diagonal + 1.0)

    for step in range(sweeps):
        picked = order_ref[step, slab]
        after = jnp.where(block_of == picked, jnp.maximum(current + wanted * rate, 0.0), current)
        if step < sweeps - 1:
            moved = after - current
            block = jnp.zeros((BLOCK, frames_here), f32)
            for k in range(sweeps):
                block = jnp.where(picked == k, moved[k * BLOCK : (k + 1) * BLOCK], block)
            blk_out[step] = block
            for offset in OFFSETS:
                start(functools.partial(send_block, step), offset)
            change[2 * width : 3 * width, :] = moved
            for offset in OFFSETS:
                arrive(functools.partial(send_block, step), offset)
            for offset in OFFSETS:
                there = jnp.clip(slab + offset, 0, owners - 1)
                first = (2 + offset) * width
                news = jnp.concatenate([blk_in[step, slot(offset)]] * sweeps, axis=0)
                change[first : first + width, :] = jnp.where(block_of == order_ref[step, there], news, 0.0)
            high, low = halves(change[...])
            for i in range(3):
                span = slice(i * width, i * width + three)
                both = dot(stacked[i], high[span])
                wanted -= both[:width] + both[width:] + dot(tops[i], low[span])
        current = after
    near[width : 2 * width, :] = current.astype(bf16)
    for offset in (-1, 1):
        start(send_near, offset)
    for d in range(1, shares):
        send_far(d).start()
    updated_ref[...] = current
    pltpu.make_async_copy(updated_ref, updated_hbm, out_sem.at[whole_pieces + part_pieces]).start()

    for offset in (-1, 1):
        arrive(send_near, offset)
    traces_near = near[...]
    over_frames = ((1,), (1,))
    gram_here = dot(traces_near, traces_near, over_frames)
    both_here = jnp.concatenate(halves(gram_here), axis=0)

    def residual(first):
        rows = pl.ds(first, rows_each)
        fitted = dot(both_here, act[:, rows])
        return dot(traces_near, frames_ref[rows, :], over_frames) - fitted[:three] - fitted[three:]

    for piece in range(part_pieces):
        for d in range(1, shares):
            part_out[d - 1, piece] = residual(first_of(partner(d), whole_pieces + piece)).astype(bf16)
            send_part(d, piece).start()
        if piece == 0:
            for d in range(1, shares):
                send_far(d).wait_recv()
                for offset in (-1, 1):
                    start(functools.partial(relay, d), offset)
    for piece in range(part_pieces):
        part_own[piece] = residual(first_of(mine, whole_pieces + piece))

    gram = gram_here
    for d in range(1, shares):
        for offset in (-1, 1):
            arrive(functools.partial(relay, d), offset)
        gram += dot(near_far[d - 1], near_far[d - 1], over_frames)
    grow = lax.broadcasted_iota(jnp.int32, (three, three), 0)
    gcol = lax.broadcasted_iota(jnp.int32, (three, three), 1)
    rate = 1.0 / (jnp.sum(jnp.where(grow == gcol, gram, 0.0), axis=1, keepdims=True) + 1.0)
    gram_high, gram_low = halves(gram)
    gram_both = jnp.concatenate([gram_high, gram_low], axis=0)
    line_block = lax.rem(line, width) // BLOCK
    picks = []
    for step in range(sweeps):
        chosen = [order_ref[step, jnp.clip(slab - 1 + w, 0, owners - 1)] for w in range(3)]
        chosen = jnp.where(window_of == 0, chosen[0], jnp.where(window_of == 1, chosen[1], chosen[2]))
        picks.append(line_block == chosen)

    def deposit(piece):
        span = pl.ds(piece * rows_each, rows_each)
        return pltpu.make_async_copy(refined_ref.at[:, span], refined_hbm.at[:, span], out_sem.at[piece])

    def refine(piece, left_over):
        here = pl.ds(first_of(mine, piece), rows_each)
        shaped = act[:, here].astype(f32)
        mask = keep[:, here].astype(f32)
        for step in range(sweeps):
            after = jnp.where(picks[step], jnp.maximum(shaped + left_over * rate, 0.0) * mask, shaped)
            if step < sweeps - 1:
                moved, rest = halves(after - shaped)
                lost = dot(gram_both, moved)
                left_over = left_over - (lost[:three] + lost[three:] + dot(gram_high, rest))
            shaped = after
        refined_ref[:, piece * rows_each : (piece + 1) * rows_each] = shaped.astype(bf16)
        deposit(piece).start()

    for piece in range(whole_pieces):
        here = pl.ds(first_of(mine, piece), rows_each)
        fitted = dot(gram_both, act[:, here])
        left_over = dot(traces_near, frames_ref[here, :], over_frames) - fitted[:three] - fitted[three:]
        for d in range(1, shares):
            send_frames(d, piece).wait_recv()
            left_over += dot(near_far[d - 1], frames_in[d - 1, piece], over_frames)
        refine(piece, left_over)
    for piece in range(part_pieces):
        left_over = part_own[piece]
        for d in range(1, shares):
            send_part(d, piece).wait_recv()
            left_over += part_in[d - 1, piece].astype(f32)
        refine(whole_pieces + piece, left_over)

    for piece in range(whole_pieces + part_pieces):
        deposit(piece).wait()
    pltpu.make_async_copy(updated_ref, updated_hbm, out_sem.at[whole_pieces + part_pieces]).wait()
    for offset in OFFSETS:
        for step in range(sweeps - 1):
            left(functools.partial(send_block, step), offset)
    for offset in (-1, 1):
        for copy in (send_traces, send_drive, send_corr, send_near):
            left(copy, offset)
        for d in range(1, shares):
            left(functools.partial(relay, d), offset)
    for d in range(1, shares):
        send_far(d).wait_send()
        for piece in range(whole_pieces):
            send_frames(d, piece).wait_send()
        for piece in range(part_pieces):
            send_part(d, piece).wait_send()


def deliver_kernel(refined_ref, updated_ref, refined_out, updated_out, refined_held, updated_held, sem):
    rows = refined_ref.shape[0] // 4
    moves = [(updated_ref, updated_held, updated_out)]
    for i in range(4):
        part = pl.ds(i * rows, rows)
        moves.append((refined_ref.at[part], refined_held.at[part], refined_out.at[part]))
    inward = [pltpu.make_async_copy(a, b, sem.at[0, i]) for i, (a, b, c) in enumerate(moves)]
    outward = [pltpu.make_async_copy(b, c, sem.at[1, i]) for i, (a, b, c) in enumerate(moves)]
    for copy in inward:
        copy.start()
    for copy, onward in zip(inward, outward):
        copy.wait()
        onward.start()
    for copy in outward:
        copy.wait()


def deliver(refined, updated):
    like = [jax.ShapeDtypeStruct(x.shape, x.dtype) for x in (refined, updated)]
    anywhere = pl.BlockSpec(memory_space=pl.ANY)
    refined, updated = pl.pallas_call(
        deliver_kernel, out_shape=like, in_specs=[anywhere] * 2, out_specs=[anywhere] * 2,
        scratch_shapes=[pltpu.VMEM(x.shape, x.dtype) for x in like] + [pltpu.SemaphoreType.DMA((2, 5))],
        compiler_params=pltpu.CompilerParams(vmem_limit_bytes=56 * 1024 * 1024),
    )(refined, updated)
    return refined.T, updated


def shards(owners, shares, frames, footprints, support, traces, block_order):
    pixels, frames_here = frames.shape
    width = traces.shape[0]
    three = 3 * width
    rounds = max(width // BLOCK - 1, 1)
    share_rows = pixels // shares
    rows_each = min(share_rows // 2, 128)
    pieces = share_rows // rows_each
    whole_pieces = max(pieces * WHOLE // 16, 1)
    part_pieces = pieces - whole_pieces
    others = max(shares - 1, 1)
    groups = 4
    vmem, dma = pltpu.VMEM, pltpu.SemaphoreType.DMA
    refined, updated = pl.pallas_call(
        functools.partial(kernel, owners, shares),
        out_shape=(
            jax.ShapeDtypeStruct((three, share_rows), bf16),
            jax.ShapeDtypeStruct(traces.shape, f32),
        ),
        in_specs=[pl.BlockSpec(memory_space=pl.ANY)] * 5,
        out_specs=(pl.BlockSpec(memory_space=pl.ANY), pl.BlockSpec(memory_space=pl.ANY)),
        scratch_shapes=[
            pltpu.SMEM(block_order.shape[::-1], jnp.int32),
            vmem(frames.shape, bf16),
            vmem(support.shape[::-1], jnp.int32),
            vmem((three, pixels), bf16),
            vmem((three, pixels), bf16),
            vmem((three, frames_here), f32),
            vmem((three, frames_here), f32),
            vmem((three, three), f32),
            vmem((2, width, frames_here), f32),
            vmem((2, width, three), f32),
            vmem((5 * width, frames_here), f32),
            vmem((rounds, BLOCK, frames_here), f32),
            vmem((rounds, 4, BLOCK, frames_here), f32),
            vmem((three, frames_here), bf16),
            vmem((others, three, frames_here), bf16),
            vmem((others, whole_pieces, rows_each, frames_here), bf16),
            vmem((part_pieces, three, rows_each), f32),
            vmem((others, part_pieces, three, rows_each), bf16),
            vmem((others, part_pieces, three, rows_each), bf16),
            vmem((three, share_rows), bf16), vmem(traces.shape, f32), dma((pieces + 1,)),
            dma((groups + 1, 2)), dma,
            dma((2,)), dma((2,)), dma((2,)), dma((2,)), dma((2,)), dma((2,)),
            dma((rounds, 4)), dma((rounds, 4)), dma((2,)), dma((2,)),
            dma((others,)), dma((others,)), dma((others, 2)), dma((others, 2)),
            dma((others, whole_pieces)), dma((others, whole_pieces)),
            dma((others, part_pieces)), dma((others, part_pieces)),
        ],
        compiler_params=pltpu.CompilerParams(
            collective_id=0, has_side_effects=True, vmem_limit_bytes=56 * 1024 * 1024
        ),
    )(block_order.T, frames, footprints.T, support.T, traces)
    return deliver(refined, updated)


def solution(mesh):
    in_specs = (P("pix", "frm"), P("pix", None), P("pix", None), P("pix", "frm"), P())
    out_specs = (P(("pix", "frm"), None), P("pix", "frm"))
    body = functools.partial(shards, mesh.shape["pix"], mesh.shape["frm"])
    return jax.shard_map(body, mesh=mesh, in_specs=in_specs, out_specs=out_specs, check_vma=False)
```
